256 devices in a mesh: node: 64 (over z, x, core), feat: 4 (over y).
Axes of the slice: x: 4, y: 4, z: 8, core: 2. Of those that a mesh axis runs over, the one named last changes fastest.
Arguments:
- features: float32 [49152, 1024], P('node', 'feat'), may hold values from -6 to 6
- degrees: int32 [49152], P('node'), may hold values from 1 to 4
- tile_row: int32 [64, 201], P('node'), may hold values from 0 to 5, as said below
- tile_col: int32 [64, 201], P('node'), may hold values from 0 to 69, as said below
- tile_count: int32 [64], P('node'), may hold values from 75 to 201, as said below
- send_block: int32 [64, 64], replicated, may hold values from 0 to 5
- tile_val: bfloat16 [64, 201, 128, 128], P('node'), may hold values from -0.15625 to 0.15625
- weight: bfloat16 [1024, 3, 1024], P('node', None, 'feat'), may hold values from -0.109375 to 0.109375
- out_bias: float32 [1024], replicated, may hold values from -3 to 3
- cotangent: bfloat16 [49152, 1024], P(('node', 'feat')), may hold values from -0.109375 to 0.109375
Outputs:
- output: bfloat16 [49152, 1024], P(('node', 'feat'))
- weight_grad: float32 [1024, 3, 1024], P('node', None, 'feat')
- bias_grad: float32 [1024], replicated
The draws below stay inside these ranges and needn't reach their ends.
Inputs may be any that keep to these rules, and one draw needn't show every extreme that they name: `tile_row`: the row block of each slot; for each other part q, between 1 and 3 live tiles of part p read slot 6 + q, each at a different row block. `tile_col`: below 6: the part's own row block; 6 + q: the block that part q sends; the first 12 slots of each part read own blocks, tile i < 6 at row block i, column i; slots past tile_count read 0; no tile reads slot 6 + p in part p. `tile_count`: live tiles come first in each part; some part has 201 live tiles.
All inputs are finite; a program needn't handle non-finite values.
Results may differ from the reference program's by a relative error of at most 0.0057.
Values may be sent and summed in bfloat16 or wider, within the bound.
No kernel may reach another device: no remote copies, remote signals or barrier semaphores. Data moves between devices by JAX's collectives and lax.ppermute only.
A program may use at most 192 MiB of HBM per device.

```python
import jax
import jax.numpy as jnp
from jax import lax

F = 1024
OUT = 1024
HOPS = 2
BLOCK = 128
RB = 6
MULT = 3
PARTS_SIZE = 64
NBLOCKS = 384
NODES = 49152
TILES_DEV = 201


def graph_tables(key):
    key = jax.random.fold_in(key, 4242)
    keys = jax.random.split(key, 5)
    send_block = jax.random.randint(keys[0], (PARTS_SIZE, PARTS_SIZE), 0, RB)
    busiest = jax.random.randint(keys[1], (), 0, PARTS_SIZE)
    level = jax.random.randint(keys[2], (PARTS_SIZE, PARTS_SIZE), 0, 10)
    multiple = jnp.where(level < 8, 1, jnp.where(level < 9, 2, MULT))
    part_ids = jnp.arange(PARTS_SIZE, dtype=jnp.int32)
    multiple = jnp.where(part_ids[:, None] == busiest, MULT, multiple)
    multiple = jnp.where(part_ids[:, None] == part_ids[None, :], 0, multiple)
    order_keys = jax.random.randint(keys[3], (PARTS_SIZE, PARTS_SIZE, RB), 0, 1 << 20) * RB + jnp.arange(RB, dtype=jnp.int32)
    row_choice = jnp.argsort(order_keys, axis=-1)[:, :, :MULT].astype(jnp.int32)
    slot_ids = jnp.arange(MULT, dtype=jnp.int32)
    valid = slot_ids[None, None, :] < multiple[:, :, None]
    flat_valid = valid.reshape(PARTS_SIZE, PARTS_SIZE * MULT)
    flat_rows = row_choice.reshape(PARTS_SIZE, PARTS_SIZE * MULT)
    flat_source = jnp.broadcast_to(part_ids[None, :, None], (PARTS_SIZE, PARTS_SIZE, MULT)).reshape(PARTS_SIZE, PARTS_SIZE * MULT)
    rank = jnp.where(flat_valid, 0, 1) * (PARTS_SIZE * MULT) + jnp.arange(PARTS_SIZE * MULT, dtype=jnp.int32)
    picked = jnp.argsort(rank, axis=-1)[:, :MULT * (PARTS_SIZE - 1)]
    remote_valid = jnp.take_along_axis(flat_valid, picked, axis=1)
    remote_row = jnp.where(remote_valid, jnp.take_along_axis(flat_rows, picked, axis=1), 0)
    remote_col = jnp.where(remote_valid, RB + jnp.take_along_axis(flat_source, picked, axis=1), 0)
    own_ids = jnp.broadcast_to(jnp.arange(RB, dtype=jnp.int32)[None, :], (PARTS_SIZE, RB))
    offset = jax.random.randint(keys[4], (PARTS_SIZE, RB), 1, RB)
    local_row = jnp.concatenate([own_ids, own_ids], axis=1)
    local_col = jnp.concatenate([own_ids, (own_ids + offset) % RB], axis=1)
    tile_row = jnp.concatenate([local_row, remote_row], axis=1).astype(jnp.int32)
    tile_col = jnp.concatenate([local_col, remote_col], axis=1).astype(jnp.int32)
    tile_count = (2 * RB + jnp.sum(multiple, axis=1)).astype(jnp.int32)
    return (tile_row, tile_col, tile_count, send_block.astype(jnp.int32))


def draw_tile_row(key, part):
    return graph_tables(key)[0]


def draw_tile_col(key, part):
    return graph_tables(key)[1]


def draw_tile_count(key, part):
    return graph_tables(key)[2]


def draw_send_block(key, part):
    return graph_tables(key)[3]


def with_ends(values, own_key, least, top_value):
    place = [jax.random.randint(jax.random.fold_in(own_key, axis), (), 0, length) for axis, length in enumerate(values.shape)]
    widest = values.shape.index(max(values.shape))
    next_to = place[:widest] + [(place[widest] + 1) % values.shape[widest]] + place[widest + 1:]
    return values.at[tuple(place)].set(least).at[tuple(next_to)].set(top_value)


def raised(entries, stream_key, source, target, parts, factor):
    def block_of(axis_at):
        return (jnp.arange(entries.shape[axis_at]) // (entries.shape[axis_at] // parts)).reshape((-1,) + (1,) * (entries.ndim - 1 - axis_at))

    one_side = jax.random.permutation(stream_key, parts)[block_of(target)]
    second = (block_of(target) + parts // 2) % parts
    return jnp.where((block_of(source) == one_side) | (block_of(source) == second), factor * entries, entries)


def block_scale(rng, extent, cuts, low, high):
    def one(dim, shards_of):
        draws = jax.random.uniform(jax.random.fold_in(jax.random.fold_in(rng, 6), dim), (shards_of,), jnp.float32, low / len(cuts), high / len(cuts))
        return jnp.repeat(jnp.exp(draws), extent[dim] // shards_of).reshape((-1,) + (1,) * (len(extent) - dim - 1))

    level = one(*cuts[0])
    for cut in cuts[1:]:
        level = level * one(*cut)
    return level


def bell_draw(key, extent, scale, limit, pieces=(), kind=jnp.bfloat16):
    entries = scale * jax.random.normal(key, extent, jnp.float32)
    if pieces:
        entries = entries * block_scale(key, extent, pieces, -0.22, 0.18)
    return jnp.clip(entries, -limit, limit).astype(kind)


def noise_with(stream_key, shape, scale, bound, shards, heavy, held_as=jnp.bfloat16):
    values = scale * jax.random.normal(stream_key, shape, jnp.float32)
    if shards:
        values = values * block_scale(stream_key, shape, shards, -0.22, 0.18)
    return jnp.clip(raised(values, jax.random.fold_in(stream_key, 3), *heavy), -bound, bound).astype(held_as)


def setup_inputs(seed: int = 0) -> dict:
    key_of = jax.random.split(jax.random.key(seed), 11)
    return {
        "features": bell_draw(key_of[0], (NODES, F), 1.0, 6.0, ((0, 64), (1, 4)), jnp.float32),
        "degrees": with_ends(jax.random.randint(key_of[1], (NODES,), 1, 5), jax.random.fold_in(key_of[1], 1), 1, 4).astype(jnp.int32),
        "tile_row": draw_tile_row(jax.random.fold_in(key_of[10], 71), 0),
        "tile_col": draw_tile_col(jax.random.fold_in(key_of[10], 71), 0),
        "tile_count": draw_tile_count(jax.random.fold_in(key_of[10], 71), 0),
        "send_block": draw_send_block(jax.random.fold_in(key_of[10], 71), 0),
        "tile_val": bell_draw(key_of[6], (PARTS_SIZE, TILES_DEV, BLOCK, BLOCK), (2 * RB * BLOCK) ** -0.5, 0.15625, ((0, 64),)),
        "weight": bell_draw(key_of[7], (OUT, HOPS + 1, F), ((HOPS + 1) * F) ** -0.5, 0.109375, ((0, 64), (2, 4))),
        "out_bias": bell_draw(key_of[8], (OUT,), 0.5, 3.0, (), jnp.float32),
        "cotangent": noise_with(key_of[9], (NODES, OUT), (NODES ** -0.5), 0.109375, ((0, 256),), (0, 1, 256, 6.0)),
    }


def hop_product(source_blocks, tile_row, tile_col, tile_val, tile_count, send_block):
    part_ids = jnp.arange(PARTS_SIZE, dtype=jnp.int32)
    block_ids = jnp.arange(RB, dtype=jnp.int32)

    def one_part(items):
        part, row_ids, col_ids, values, live_count, received = items
        sender = jnp.clip(col_ids - RB, 0, PARTS_SIZE - 1).astype(jnp.int32)
        global_col = jnp.where(col_ids < RB, part * RB + col_ids, sender * RB + received[sender]).astype(jnp.int32)
        picked = source_blocks[global_col].astype(jnp.float32)
        product = jnp.einsum('tij,tjc->tic', values.astype(jnp.float32), picked)
        is_live = jnp.arange(row_ids.shape[0], dtype=jnp.int32) < live_count
        onehot = ((row_ids[:, None] == block_ids[None, :]) & is_live[:, None]).astype(jnp.float32)
        return jnp.einsum('tr,tic->ric', onehot, product, precision=lax.Precision.HIGHEST)
    return lax.map(one_part, (part_ids, tile_row, tile_col, tile_val, tile_count, send_block.T))

def reference(features, degrees, tile_row, tile_col, tile_count, send_block, tile_val, weight, out_bias, cotangent):
    row_scale = lax.rsqrt(degrees.astype(jnp.float32))[:, None]
    source = (features * row_scale).astype(jnp.bfloat16)
    hop_list = [features.astype(jnp.bfloat16)]
    for hop_number in range(HOPS):
        summed = hop_product(source.reshape(NBLOCKS, BLOCK, F), tile_row, tile_col, tile_val, tile_count, send_block)
        summed = summed.reshape(NODES, F)
        hop_list.append((summed * row_scale).astype(jnp.bfloat16))
        if hop_number + 1 < HOPS:
            source = (summed * row_scale * row_scale).astype(jnp.bfloat16)
    stacked = jnp.stack(hop_list, axis=1).reshape(NODES, (HOPS + 1) * F)
    flat_weight = weight.reshape(OUT, (HOPS + 1) * F)
    linear = lax.dot_general(stacked, flat_weight, (((1,), (1,)), ((), ())), preferred_element_type=jnp.float32)
    linear = linear + out_bias[None, :]
    sigmoid_val = jax.nn.sigmoid(linear)
    output = (linear * sigmoid_val).astype(jnp.bfloat16)
    grad_linear = (cotangent.astype(jnp.float32) * sigmoid_val * (1.0 + linear * (1.0 - sigmoid_val))).astype(jnp.bfloat16)
    weight_grad = lax.dot_general(grad_linear, stacked, (((0,), (0,)), ((), ())), preferred_element_type=jnp.float32)
    weight_grad = weight_grad.reshape(OUT, HOPS + 1, F)
    bias_grad = lax.optimization_barrier(jnp.sum(grad_linear.astype(jnp.float32), axis=0))
    return (output, weight_grad, bias_grad)
```

```python
import functools

import jax
import jax.numpy as jnp
from jax import lax
from jax.experimental import pallas as pl
from jax.experimental.pallas import tpu as pltpu
from jax.sharding import Mesh
from jax.sharding import PartitionSpec as P

HOPS = 2
GROUP = 8
Z = "node_0"
XC = ("node_1", "node_2")
NODE = ("node_0", "node_1", "node_2")
NODE_FEAT = ("node_0", "node_1", "node_2", "feat")


def dense_body(rows, slots, count, values, out):
    block = values.shape[-1]

    def clear(slot, carry):
        out[slot] = jnp.zeros_like(out[slot])
        return carry

    lax.fori_loop(0, out.shape[0], clear, 0)

    def step(tile, carry):
        place = (slots[tile], pl.ds(pl.multiple_of(rows[tile] * block, block), block), slice(None))
        out[place] = out[place] + values[tile]
        return carry

    lax.fori_loop(0, count[0], step, 0)


def densify(tile_rows, slots, count, tile_values, slot_total, row_total):
    block = tile_values.shape[-1]
    smem = pl.BlockSpec(memory_space=pltpu.SMEM)
    return pl.pallas_call(
        dense_body,
        out_shape=jax.ShapeDtypeStruct((slot_total, row_total, block), tile_values.dtype),
        in_specs=[smem, smem, smem, pl.BlockSpec(memory_space=pltpu.VMEM)],
        out_specs=pl.BlockSpec(memory_space=pltpu.VMEM),
        compiler_params=pltpu.CompilerParams(vmem_limit_bytes=40 << 20),
        name="densify",
    )(tile_rows, slots, count, tile_values)


def pick_body(places, wanted, *refs):
    sources, out = refs[:-1], refs[-1]
    for number, place in enumerate(places):
        for target in range(out.shape[0]):
            out[target, number] = sources[number][wanted[place, target]]


def pick(places, wanted, sources):
    block, width = sources[0].shape[1:]
    vmem = pl.BlockSpec(memory_space=pltpu.VMEM)
    return pl.pallas_call(
        functools.partial(pick_body, places),
        out_shape=jax.ShapeDtypeStruct(
            (wanted.shape[1], len(places), block, width), sources[0].dtype
        ),
        in_specs=[pl.BlockSpec(memory_space=pltpu.SMEM)] + [vmem] * len(sources),
        out_specs=vmem,
        compiler_params=pltpu.CompilerParams(vmem_limit_bytes=16 << 20),
        name="pick",
    )(wanted, *sources)


def hop_stage(dense, base, own, arrived, summed, scale):
    row_total, block = dense.shape[1:]
    width = arrived.shape[-1]
    last = scale is not None
    lead = 0 if own is None else 1

    def body(*refs):
        tiles, refs = refs[0], refs[1:]
        if lead:
            mine, refs = refs[0], refs[1:]
        sources, refs = refs[0], refs[1:]
        if summed is not None:
            before, refs = refs[0], refs[1:]
        if last:
            scaling, hop, source, acc = refs
        else:
            (acc,) = refs

        def product(right):
            size = right.shape[0] // block
            left = jnp.concatenate([tiles[i] for i in range(size)], axis=1)
            return jnp.dot(left, right, preferred_element_type=jnp.float32)

        step = pl.program_id(0)
        if lead:

            @pl.when(step == 0)
            def _():
                acc[...] = product(mine[...].reshape(-1, width))

        else:

            @pl.when(step == 0)
            def _():
                acc[...] = before[...]

        @pl.when(step >= lead)
        def _():
            acc[...] += product(sources[...].reshape(-1, width))

        if last:

            @pl.when(step == pl.num_programs(0) - 1)
            def _():
                scaled = acc[...] * scaling[...]
                hop[...] = scaled.astype(hop.dtype)
                source[...] = (scaled * scaling[...]).astype(source.dtype)

    flat = pl.BlockSpec((row_total, width), lambda i: (0, 0))
    operands, in_specs = [dense], [pl.BlockSpec((GROUP, row_total, block), lambda i: (base + i, 0, 0))]
    if lead:
        operands.append(own)
        in_specs.append(pl.BlockSpec(own.shape, lambda i: (0, 0, 0)))
    operands.append(arrived)
    in_specs.append(
        pl.BlockSpec((arrived.shape[0], 1, block, width), lambda i: (0, jnp.maximum(i - lead, 0), 0, 0))
    )
    if summed is not None:
        operands.append(summed)
        in_specs.append(flat)
    total = jax.ShapeDtypeStruct((row_total, width), jnp.float32)
    rounded = jax.ShapeDtypeStruct((row_total, width), jnp.bfloat16)
    if last:
        operands.append(scale)
        in_specs.append(flat)
    return pl.pallas_call(
        body,
        grid=(arrived.shape[1] + lead,),
        out_shape=(rounded, rounded) if last else total,
        in_specs=in_specs,
        out_specs=(flat, flat) if last else flat,
        scratch_shapes=[pltpu.VMEM((row_total, width), jnp.float32)] if last else [],
        compiler_params=pltpu.CompilerParams(vmem_limit_bytes=40 << 20),
        name="hop_last" if last else "hop_stage",
    )(*operands)


def shift(array, axis, step):
    length = lax.axis_size(axis)
    return lax.ppermute(array, axis, [(i, (i + step) % length) for i in range(length)])


def propagate(source, dense, wanted, scale, block):
    _, width = source.shape
    along = lax.axis_size(Z)
    own = source.reshape(-1, block, width)
    half = own.shape[0] // 2

    def exchange(places, sources):
        outgoing = pick(places, wanted, sources)
        return lax.all_to_all(outgoing, XC, split_axis=0, concat_axis=0, tiled=True)

    arrived = [exchange([0], [own])]
    low, high = own, own
    far = along // 2
    for distance in range(1, far):
        low, high = shift(low, Z, 1), shift(high, Z, -1)
        if distance < far - 1:
            arrived.append(exchange([distance, along - distance], [high, low]))
    opposite = [shift(low[:half], Z, 1), shift(high[half:], Z, -1)]
    opposite = jnp.concatenate(opposite, axis=0)
    places = [far - 1, along - far + 1, far]
    arrived.append(exchange(places, [high, low, opposite]))
    summed = hop_stage(dense, 0, own, arrived[0], None, None)
    summed = hop_stage(dense, 2, None, arrived[1], summed, None)
    summed = hop_stage(dense, 4, None, arrived[2], summed, None)
    return hop_stage(dense, 6, None, arrived[3], summed, scale)


def at(array, index):
    return lax.dynamic_index_in_dim(array, index % array.shape[0], 0, keepdims=False)


def ring_sum(pieces, axis):
    opposite, following, leading, mine = pieces
    half = opposite.shape[0] // 2
    opposite = opposite.astype(jnp.bfloat16)
    up, down = shift(opposite[:half], axis, 1), shift(opposite[half:], axis, -1)
    up, down = up.astype(jnp.float32), down.astype(jnp.float32)
    following = jnp.concatenate([following[:half] + up, following[half:]]).astype(jnp.bfloat16)
    leading = jnp.concatenate([leading[:half], leading[half:] + down]).astype(jnp.bfloat16)
    up, down = shift(following, axis, 1), shift(leading, axis, -1)
    return mine + up.astype(jnp.float32) + down.astype(jnp.float32)


def layer(features, hops, flat_weight, weight, out_bias, cotangent):
    rows, along = features.shape[0], lax.axis_size(Z)
    panels = lax.axis_size("feat")
    feat_index = lax.axis_index("feat")
    flat_rows = jnp.concatenate([features.astype(jnp.bfloat16)] + hops, axis=1)
    by_owner = flat_rows.reshape(panels, rows // panels, -1)
    near = [at(by_owner, feat_index + i) for i in range(panels)]

    def term_of(owner_rows):
        return lax.dot_general(
            owner_rows, flat_weight, (((1,), (1,)), ((), ())), preferred_element_type=jnp.float32
        )

    linear = ring_sum([term_of(near[2]), term_of(near[1]), term_of(near[3]), term_of(near[0])], "feat")
    linear = linear + out_bias[None, :]
    sigmoid_val = jax.nn.sigmoid(linear)
    output = (linear * sigmoid_val).astype(jnp.bfloat16)
    grad_linear = (
        cotangent.astype(jnp.float32) * sigmoid_val * (1.0 + linear * (1.0 - sigmoid_val))
    ).astype(jnp.bfloat16)

    bias = jnp.sum(grad_linear.astype(jnp.float32), axis=0)
    for axes in (("node_1", "node_2", "feat"), Z):
        copies = jnp.broadcast_to(bias[None], (lax.axis_size(axes), bias.shape[0]))
        copies = lax.all_to_all(copies, axes, 0, 0, tiled=True)
        bias = jnp.sum(copies, axis=0)

    half = grad_linear.shape[0] // 2
    up, down = shift(grad_linear, "feat", 1), shift(grad_linear, "feat", -1)
    opposite = [shift(up[:half], "feat", 1), shift(down[half:], "feat", -1)]
    opposite = jnp.concatenate(opposite)

    def outer(grads, owner_rows):
        return lax.dot_general(
            grads, owner_rows, (((0,), (0,)), ((), ())), preferred_element_type=jnp.float32
        )

    term = outer(jnp.concatenate([grad_linear, up, down]), jnp.concatenate([near[0], near[3], near[1]]))
    term = term + outer(opposite, near[2])
    columns = term.shape[1]
    term = term.reshape(along, 4, 2, weight.shape[0], columns)
    term = jnp.moveaxis(term, (2, 1), (0, 1))
    core = lax.axis_index("node_2")
    other = shift(at(term, core + 1).astype(jnp.bfloat16), "node_2", 1)
    term = (at(term, core) + other.astype(jnp.float32)).reshape(4, -1, columns)
    x_index = lax.axis_index("node_1")
    term = ring_sum([at(term, x_index + i) for i in (2, 1, 3, 0)], "node_1")
    term = term.astype(jnp.bfloat16).reshape(along, -1, columns)
    term = lax.all_to_all(term, Z, 0, 0, tiled=True)
    weight_grad = jnp.sum(term.astype(jnp.float32), axis=0).reshape(weight.shape)
    return (output, weight_grad, bias)


def local(
    features,
    degrees,
    tile_row,
    tile_col,
    tile_count,
    send_block,
    tile_val,
    weight,
    out_bias,
    cotangent,
):
    rows, panel = features.shape
    block = tile_val.shape[-1]
    row_blocks = rows // block
    parts = send_block.shape[0]
    along = lax.axis_size(Z)
    across = parts // along
    z_index = lax.axis_index(Z)
    xc_index = lax.axis_index(XC)

    flat_weight = lax.all_gather(weight.reshape(weight.shape[0], -1), NODE, axis=0, tiled=True)
    row_scale = lax.rsqrt(degrees.astype(jnp.float32))[:, None]
    source = (features * row_scale).astype(jnp.bfloat16)
    scale = jnp.broadcast_to(row_scale, (rows, panel))

    by_place = send_block.reshape(along, across, along, across)
    mine = lax.dynamic_index_in_dim(by_place, xc_index, 1, keepdims=False)
    mine = lax.dynamic_index_in_dim(mine, z_index, 1, keepdims=False)
    wanted = jnp.roll(mine, -z_index, axis=0)

    order = [0]
    for distance in range(1, along // 2):
        order += [distance, along - distance]
    order.append(along // 2)
    place_of = jnp.array([order.index(offset) for offset in range(along)], dtype=jnp.int32)
    sender = jnp.maximum(tile_col[0] - row_blocks, 0)
    offset = (sender // across - z_index) % along
    remote = GROUP + place_of[offset] * across + sender % across
    slots = jnp.where(tile_col[0] < row_blocks, tile_col[0], remote)
    dense = densify(tile_row[0], slots, tile_count, tile_val[0], GROUP + parts, rows)

    hops = []
    for _ in range(HOPS):
        hop, source = propagate(source, dense, wanted, scale, block)
        hops.append(hop)

    args = (features, hops, flat_weight, weight, out_bias, cotangent)
    return layer(*args)


def solution(mesh):
    split = Mesh(
        mesh.devices.reshape(8, 4, 2, mesh.shape["feat"]), ("node_0", "node_1", "node_2", "feat")
    )
    return jax.shard_map(
        local,
        mesh=split,
        in_specs=(
            P(NODE, "feat"),
            P(NODE),
            P(NODE, None),
            P(NODE, None),
            P(NODE),
            P(),
            P(NODE, None, None, None),
            P(NODE, None, "feat"),
            P(),
            P(NODE_FEAT, None),
        ),
        out_specs=(P(NODE_FEAT, None), P(NODE, None, "feat"), P()),
        check_vma=False,
    )
```

```python
import functools

import jax
import jax.numpy as jnp
from jax import lax
from jax.experimental import pallas as pl
from jax.experimental.pallas import tpu as pltpu
from jax.sharding import Mesh
from jax.sharding import PartitionSpec as P

GROUP = 8
SPLIT = 1
Z = "node_0"
XC = ("node_1", "node_2")
NODE = ("node_0", "node_1", "node_2")
NODE_FEAT = ("node_0", "node_1", "node_2", "feat")


def dense_body(rows, slots, count, values, out):
    block = values.shape[-1]

    def clear(slot, carry):
        out[slot] = jnp.zeros_like(out[slot])
        return carry

    lax.fori_loop(0, out.shape[0], clear, 0)

    def step(tile, carry):
        place = (slots[tile], pl.ds(pl.multiple_of(rows[tile] * block, block), block), slice(None))
        out[place] = out[place] + values[tile]
        return carry

    lax.fori_loop(0, count[0], step, 0)


def densify(tile_rows, slots, count, tile_values, slot_total, row_total):
    block = tile_values.shape[-1]
    smem = pl.BlockSpec(memory_space=pltpu.SMEM)
    return pl.pallas_call(
        dense_body,
        out_shape=jax.ShapeDtypeStruct((slot_total, row_total, block), tile_values.dtype),
        in_specs=[smem, smem, smem, pl.BlockSpec(memory_space=pltpu.VMEM)],
        out_specs=pl.BlockSpec(memory_space=pltpu.VMEM),
        compiler_params=pltpu.CompilerParams(vmem_limit_bytes=40 << 20),
        name="densify",
    )(tile_rows, slots, count, tile_values)


def pick_body(places, pairs, wanted, *refs):
    *sources, out, done = refs
    targets = out.shape[0]
    copies = []
    for number, place in enumerate(places):
        first = sources.pop(0)
        second = sources.pop(0) if number in pairs else None
        for target in range(targets):
            index = wanted[place, target]
            sent = done.at[number * targets + target]
            into = out.at[target, number]
            if second is None:
                pltpu.make_async_copy(first.at[index], into, sent).start()
            else:
                size = first.shape[0]

                @pl.when(index < size)
                def _(first=first, index=index, into=into, sent=sent):
                    pltpu.make_async_copy(first.at[index], into, sent).start()

                @pl.when(index >= size)
                def _(second=second, index=index, size=size, into=into, sent=sent):
                    pltpu.make_async_copy(second.at[index - size], into, sent).start()

            copies.append(pltpu.make_async_copy(first.at[0], into, sent))
    for copy in copies:
        copy.wait()


def pick(places, wanted, sources):
    flat = [array for item in sources for array in (item if isinstance(item, tuple) else (item,))]
    pairs = [i for i, item in enumerate(sources) if isinstance(item, tuple)]
    block, width = flat[0].shape[1:]
    shape = (wanted.shape[1], len(places), block, width)
    return pl.pallas_call(
        functools.partial(pick_body, places, pairs),
        out_shape=pltpu.HBM(shape, flat[0].dtype),
        in_specs=[pl.BlockSpec(memory_space=pltpu.SMEM)]
        + [pl.BlockSpec(memory_space=pltpu.VMEM)] * len(flat),
        out_specs=pl.BlockSpec(memory_space=pltpu.HBM),
        scratch_shapes=[pltpu.SemaphoreType.DMA((shape[0] * shape[1],))],
        compiler_params=pltpu.CompilerParams(vmem_limit_bytes=8 << 20),
        name="pick",
    )(wanted, *flat)


def hop_stage(dense, base, own, arrived, summed, finish):
    row_total, block = dense.shape[1:]
    width = arrived.shape[-1]
    last = finish is not None
    lead = 0 if own is None else 1

    def body(*refs):
        tiles, refs = refs[:SPLIT], refs[SPLIT:]
        if lead:
            mine, refs = refs[0], refs[1:]
        sources, refs = refs[0], refs[1:]
        if summed is not None:
            before, refs = refs[0], refs[1:]
        if last:
            position, scaling, *hops, source, acc = refs
        else:
            (acc,) = refs

        def product(right):
            size = right.shape[0] // block
            each = GROUP // SPLIT
            left = [tiles[i // each][i % each] for i in range(size)]
            left = jnp.concatenate(left, axis=1)
            return jnp.dot(left, right, preferred_element_type=jnp.float32)

        step = pl.program_id(0)
        if lead:

            @pl.when(step == 0)
            def _():
                acc[...] = product(mine[...].reshape(-1, width))

        else:

            @pl.when(step == 0)
            def _():
                acc[...] = before[...]

        @pl.when(step >= lead)
        def _():
            acc[...] += product(sources[...].reshape(-1, width))

        if last:

            @pl.when(step == pl.num_programs(0) - 1)
            def _():
                scaled = acc[...] * scaling[...]
                source[...] = (scaled * scaling[...]).astype(source.dtype)
                acc[...] = scaled
                for number, hop in enumerate(hops):
                    size = hop.shape[0]
                    owner = (position[0] + number) % len(hops)
                    start = pl.multiple_of(owner * size, size)
                    hop[...] = acc[pl.ds(start, size), :].astype(hop.dtype)

    flat = pl.BlockSpec((row_total, width), lambda i: (0, 0))
    operands, in_specs = [dense] * SPLIT, []
    for k in range(SPLIT):
        in_specs.append(
            pl.BlockSpec(
                (GROUP // SPLIT, row_total, block), lambda i, k=k: ((base + i) * SPLIT + k, 0, 0)
            )
        )
    if lead:
        operands.append(own)
        in_specs.append(pl.BlockSpec(own.shape, lambda i: (0, 0, 0)))
    operands.append(pltpu.with_memory_space_constraint(arrived, pltpu.HBM))
    in_specs.append(
        pl.BlockSpec((arrived.shape[0], 1, block, width), lambda i: (0, jnp.maximum(i - lead, 0), 0, 0))
    )
    if summed is not None:
        operands.append(summed)
        in_specs.append(flat)
    total = jax.ShapeDtypeStruct((row_total, width), jnp.float32)
    out_shape, out_specs = total, flat
    if last:
        scale, panels = finish
        operands += [lax.axis_index("feat").astype(jnp.int32).reshape(1), scale]
        in_specs += [pl.BlockSpec(memory_space=pltpu.SMEM), flat]
        part = (row_total // panels, width)
        out_shape = [pltpu.HBM(part, jnp.bfloat16)] * panels
        out_shape.append(jax.ShapeDtypeStruct((row_total, width), jnp.bfloat16))
        out_specs = [pl.BlockSpec(part, lambda i: (0, 0))] * panels + [flat]
    return pl.pallas_call(
        body,
        grid=(arrived.shape[1] + lead,),
        out_shape=out_shape,
        in_specs=in_specs,
        out_specs=out_specs,
        scratch_shapes=[pltpu.VMEM((row_total, width), jnp.float32)] if last else [],
        compiler_params=pltpu.CompilerParams(vmem_limit_bytes=40 << 20),
        name="hop_last" if last else "hop_stage",
    )(*operands)


def shift(array, axis, step):
    length = lax.axis_size(axis)
    return lax.ppermute(array, axis, [(i, (i + step) % length) for i in range(length)])


def propagate(source, dense, wanted, scale, panels, block, cuts, beside):
    _, width = source.shape
    along = lax.axis_size(Z)
    far = along // 2
    own = source.reshape(-1, block, width)
    half = own.shape[0] // 2
    places, sources = [0], [own]
    low, high = own, own
    for distance in range(1, far):
        low, high = shift(low, Z, 1), shift(high, Z, -1)
        places += [distance, along - distance]
        sources += [high, low]
    opposite = shift(low[:half], Z, 1), shift(high[half:], Z, -1)
    places.append(far)
    sources.append(opposite)

    summed, done = None, ()
    for start, stop in zip([0] + cuts, cuts + [along]):
        outgoing = pick(places[start:stop], wanted, sources[start:stop])
        arrived = lax.all_to_all(outgoing, XC, split_axis=0, concat_axis=0, tiled=True)
        if stop == along and beside is not None:
            summed, done = lax.optimization_barrier((summed, beside()))
        base = start + 1 if start else 0
        summed = hop_stage(
            dense,
            base,
            None if start else own,
            arrived,
            summed,
            (scale, panels) if stop == along else None,
        )
    return summed, done


def gather_rows(rows):
    along, size = lax.axis_size(Z), lax.axis_size(XC)
    copies = jnp.broadcast_to(rows[None], (size, *rows.shape))
    own = lax.all_to_all(copies, XC, 0, 0, tiled=True).reshape(-1, rows.shape[1])
    position = lax.axis_index(Z)
    whole = jnp.zeros((along, *own.shape), own.dtype)

    def put(whole, piece, distance):
        return lax.dynamic_update_index_in_dim(whole, piece, (position + distance) % along, 0)

    whole = put(whole, own, 0)
    low, high = own, own
    for distance in range(1, along // 2):
        low, high = shift(low, Z, 1), shift(high, Z, -1)
        whole = put(put(whole, high, distance), low, along - distance)
    half = own.shape[0] // 2
    opposite = [shift(low[:half], Z, 1), shift(high[half:], Z, -1)]
    whole = put(whole, jnp.concatenate(opposite), along // 2)
    return whole.reshape(-1, rows.shape[1])


def at(array, index):
    return lax.dynamic_index_in_dim(array, index % array.shape[0], 0, keepdims=False)


def ring_sum(pieces, axis):
    opposite, following, leading, mine = pieces
    half = opposite.shape[0] // 2
    opposite = opposite.astype(jnp.bfloat16)
    up, down = shift(opposite[:half], axis, 1), shift(opposite[half:], axis, -1)
    up, down = up.astype(jnp.float32), down.astype(jnp.float32)
    following = jnp.concatenate([following[:half] + up, following[half:]]).astype(jnp.bfloat16)
    leading = jnp.concatenate([leading[:half], leading[half:] + down]).astype(jnp.bfloat16)
    up, down = shift(following, axis, 1), shift(leading, axis, -1)
    return mine + up.astype(jnp.float32) + down.astype(jnp.float32)


def spread(near):
    return [near[0]] + [shift(near[i], "feat", i) for i in range(1, len(near))]


def term_of(owner_rows, owner_weight):
    return lax.dot_general(
        owner_rows, owner_weight, (((1,), (1,)), ((), ())), preferred_element_type=jnp.float32
    )


def layer(near, early, first_terms, last_weight, weight, out_bias, cotangent):
    along = lax.axis_size(Z)
    wide = jnp.concatenate(spread(near[-1]), axis=1)
    linear = first_terms + term_of(wide, last_weight)
    by_owner = [
        jnp.concatenate([early[i], near[-1][i]], axis=1) for i in range(len(early))
    ]
    linear = linear + out_bias[None, :]
    sigmoid_val = jax.nn.sigmoid(linear)
    output = (linear * sigmoid_val).astype(jnp.bfloat16)
    grad_linear = (
        cotangent.astype(jnp.float32) * sigmoid_val * (1.0 + linear * (1.0 - sigmoid_val))
    ).astype(jnp.bfloat16)

    bias = jnp.sum(grad_linear.astype(jnp.float32), axis=0)
    for axes in (("node_1", "node_2", "feat"), Z):
        copies = jnp.broadcast_to(bias[None], (lax.axis_size(axes), bias.shape[0]))
        copies = lax.all_to_all(copies, axes, 0, 0, tiled=True)
        bias = jnp.sum(copies, axis=0)

    half = grad_linear.shape[0] // 2
    up, down = shift(grad_linear, "feat", 1), shift(grad_linear, "feat", -1)
    opposite = [shift(up[:half], "feat", 1), shift(down[half:], "feat", -1)]
    opposite = jnp.concatenate(opposite)

    def outer(grads, owner_rows):
        return lax.dot_general(
            grads, owner_rows, (((0,), (0,)), ((), ())), preferred_element_type=jnp.float32
        )

    term = outer(jnp.concatenate([grad_linear, up, down]), jnp.concatenate([by_owner[0], by_owner[3], by_owner[1]]))
    term = term + outer(opposite, by_owner[2])
    columns = term.shape[1]
    term = term.reshape(along, 4, 2, weight.shape[0], columns)
    core = lax.axis_index("node_2")
    mine = lax.dynamic_index_in_dim(term, core, 2, keepdims=False)
    other = jnp.moveaxis(lax.dynamic_index_in_dim(term, 1 - core, 2, keepdims=False), 1, 0)
    other = shift(other.astype(jnp.bfloat16), "node_2", 1)
    term = (jnp.moveaxis(mine, 1, 0) + other.astype(jnp.float32)).reshape(4, -1, columns)
    x_index = lax.axis_index("node_1")
    term = ring_sum([at(term, x_index + i) for i in (2, 1, 3, 0)], "node_1")
    term = term.astype(jnp.bfloat16).reshape(along, -1, columns)
    term = lax.all_to_all(term, Z, 0, 0, tiled=True)
    weight_grad = jnp.sum(term.astype(jnp.float32), axis=0).reshape(weight.shape)
    return (output, weight_grad, bias)


def local(
    features,
    degrees,
    tile_row,
    tile_col,
    tile_count,
    send_block,
    tile_val,
    weight,
    out_bias,
    cotangent,
):
    rows, panel = features.shape
    block = tile_val.shape[-1]
    row_blocks = rows // block
    parts = send_block.shape[0]
    along = lax.axis_size(Z)
    across = parts // along
    z_index = lax.axis_index(Z)
    xc_index = lax.axis_index(XC)

    panels = lax.axis_size("feat")
    feat_index = lax.axis_index("feat")
    row_scale = lax.rsqrt(degrees.astype(jnp.float32))[:, None]
    source = (features * row_scale).astype(jnp.bfloat16)
    scale = jnp.broadcast_to(row_scale, (rows, panel))

    by_place = send_block.reshape(along, across, along, across)
    mine = lax.dynamic_index_in_dim(by_place, xc_index, 1, keepdims=False)
    mine = lax.dynamic_index_in_dim(mine, z_index, 1, keepdims=False)
    wanted = jnp.roll(mine, -z_index, axis=0)

    order = [0]
    for distance in range(1, along // 2):
        order += [distance, along - distance]
    order.append(along // 2)
    place_of = jnp.array([order.index(offset) for offset in range(along)], dtype=jnp.int32)
    sender = jnp.maximum(tile_col[0] - row_blocks, 0)
    offset = (sender // across - z_index) % along
    remote = GROUP + place_of[offset] * across + sender % across
    slots = jnp.where(tile_col[0] < row_blocks, tile_col[0], remote)
    dense = densify(tile_row[0], slots, tile_count, tile_val[0], GROUP + parts, rows)

    owned = features.astype(jnp.bfloat16).reshape(panels, rows // panels, panel)
    near = [[at(owned, feat_index + i) for i in range(panels)]]
    flat_weight = gather_rows(weight.reshape(weight.shape[0], -1))
    (*hop, source), _ = propagate(source, dense, wanted, scale, panels, block, [3], None)
    near.append(hop)
    early = [jnp.concatenate([near[0][i], near[1][i]], axis=1) for i in range(panels)]
    half = flat_weight.shape[0] // 2
    up, down = shift(flat_weight, "feat", 1), shift(flat_weight, "feat", -1)
    opposite = [shift(up[:half], "feat", 1), shift(down[half:], "feat", -1)]
    by_panel = [flat_weight, up, jnp.concatenate(opposite), down]

    def beside():
        terms = 0.0
        for rows_wide, panel_weight in zip(spread(early), by_panel):
            terms = terms + term_of(rows_wide, panel_weight[:, : 2 * panel])
        last_weight = jnp.concatenate([piece[:, 2 * panel :] for piece in by_panel], axis=1)
        return terms, last_weight

    (*hop, _), (first_terms, last_weight) = propagate(
        source, dense, wanted, scale, panels, block, [3], beside
    )
    near.append(hop)

    return layer(near, early, first_terms, last_weight, weight, out_bias, cotangent)


def solution(mesh):
    split = Mesh(
        mesh.devices.reshape(8, 4, 2, mesh.shape["feat"]), ("node_0", "node_1", "node_2", "feat")
    )
    return jax.shard_map(
        local,
        mesh=split,
        in_specs=(
            P(NODE, "feat"),
            P(NODE),
            P(NODE, None),
            P(NODE, None),
            P(NODE),
            P(),
            P(NODE, None, None, None),
            P(NODE, None, "feat"),
            P(),
            P(NODE_FEAT, None),
        ),
        out_specs=(P(NODE_FEAT, None), P(NODE, None, "feat"), P()),
        check_vma=False,
    )
```

```python
import functools

import jax
import jax.numpy as jnp
from jax import lax
from jax.experimental import pallas as pl
from jax.experimental.pallas import tpu as pltpu
from jax.sharding import Mesh
from jax.sharding import PartitionSpec as P

GROUP = 8
SPLIT = 1
Z = "node_0"
XC = ("node_1", "node_2")
NODE = ("node_0", "node_1", "node_2")
NODE_FEAT = ("node_0", "node_1", "node_2", "feat")


def dense_body(rows, slots, count, values, out):
    block = values.shape[-1]

    def clear(slot, carry):
        out[slot] = jnp.zeros_like(out[slot])
        return carry

    lax.fori_loop(0, out.shape[0], clear, 0)

    def step(tile, carry):
        place = (slots[tile], pl.ds(pl.multiple_of(rows[tile] * block, block), block), slice(None))
        out[place] = out[place] + values[tile]
        return carry

    lax.fori_loop(0, count[0], step, 0)


def densify(tile_rows, slots, count, tile_values, slot_total, row_total):
    block = tile_values.shape[-1]
    smem = pl.BlockSpec(memory_space=pltpu.SMEM)
    return pl.pallas_call(
        dense_body,
        out_shape=jax.ShapeDtypeStruct((slot_total, row_total, block), tile_values.dtype),
        in_specs=[smem, smem, smem, pl.BlockSpec(memory_space=pltpu.VMEM)],
        out_specs=pl.BlockSpec(memory_space=pltpu.VMEM),
        compiler_params=pltpu.CompilerParams(vmem_limit_bytes=40 << 20),
        name="densify",
    )(tile_rows, slots, count, tile_values)


def pick_body(places, pairs, wanted, *refs):
    *sources, out, done = refs
    targets = out.shape[0]
    copies = []
    for number, place in enumerate(places):
        first = sources.pop(0)
        second = sources.pop(0) if number in pairs else None
        for target in range(targets):
            index = wanted[place, target]
            sent = done.at[number * targets + target]
            into = out.at[target, number]
            if second is None:
                pltpu.make_async_copy(first.at[index], into, sent).start()
            else:
                size = first.shape[0]

                @pl.when(index < size)
                def _(first=first, index=index, into=into, sent=sent):
                    pltpu.make_async_copy(first.at[index], into, sent).start()

                @pl.when(index >= size)
                def _(second=second, index=index, size=size, into=into, sent=sent):
                    pltpu.make_async_copy(second.at[index - size], into, sent).start()

            copies.append(pltpu.make_async_copy(first.at[0], into, sent))
    for copy in copies:
        copy.wait()


def pick(places, wanted, sources):
    flat = [array for item in sources for array in (item if isinstance(item, tuple) else (item,))]
    pairs = [i for i, item in enumerate(sources) if isinstance(item, tuple)]
    block, width = flat[0].shape[1:]
    shape = (wanted.shape[1], len(places), block, width)
    return pl.pallas_call(
        functools.partial(pick_body, places, pairs),
        out_shape=pltpu.HBM(shape, flat[0].dtype),
        in_specs=[pl.BlockSpec(memory_space=pltpu.SMEM)]
        + [pl.BlockSpec(memory_space=pltpu.VMEM)] * len(flat),
        out_specs=pl.BlockSpec(memory_space=pltpu.HBM),
        scratch_shapes=[pltpu.SemaphoreType.DMA((shape[0] * shape[1],))],
        compiler_params=pltpu.CompilerParams(vmem_limit_bytes=8 << 20),
        name="pick",
    )(wanted, *flat)


def hop_stage(dense, base, own, arrived, summed, finish):
    row_total, block = dense.shape[1:]
    width = arrived.shape[-1]
    last = finish is not None
    lead = 0 if own is None else 1

    def body(*refs):
        tiles, refs = refs[:SPLIT], refs[SPLIT:]
        if lead:
            mine, refs = refs[0], refs[1:]
        sources, refs = refs[0], refs[1:]
        if summed is not None:
            before, refs = refs[0], refs[1:]
        if last:
            position, scaling, *hops, source, acc = refs
        else:
            (acc,) = refs

        def product(right):
            size = right.shape[0] // block
            each = GROUP // SPLIT
            left = [tiles[i // each][i % each] for i in range(size)]
            left = jnp.concatenate(left, axis=1)
            return jnp.dot(left, right, preferred_element_type=jnp.float32)

        step = pl.program_id(0)
        if lead:

            @pl.when(step == 0)
            def _():
                acc[...] = product(mine[...].reshape(-1, width))

        else:

            @pl.when(step == 0)
            def _():
                acc[...] = before[...]

        @pl.when(step >= lead)
        def _():
            acc[...] += product(sources[...].reshape(-1, width))

        if last:

            @pl.when(step == pl.num_programs(0) - 1)
            def _():
                scaled = acc[...] * scaling[...]
                source[...] = (scaled * scaling[...]).astype(source.dtype)
                acc[...] = scaled
                for number, hop in enumerate(hops):
                    size = hop.shape[0]
                    owner = (position[0] + number) % len(hops)
                    start = pl.multiple_of(owner * size, size)
                    hop[...] = acc[pl.ds(start, size), :].astype(hop.dtype)

    flat = pl.BlockSpec((row_total, width), lambda i: (0, 0))
    operands, in_specs = [dense] * SPLIT, []
    for k in range(SPLIT):
        in_specs.append(
            pl.BlockSpec(
                (GROUP // SPLIT, row_total, block), lambda i, k=k: ((base + i) * SPLIT + k, 0, 0)
            )
        )
    if lead:
        operands.append(own)
        in_specs.append(pl.BlockSpec(own.shape, lambda i: (0, 0, 0)))
    operands.append(pltpu.with_memory_space_constraint(arrived, pltpu.HBM))
    in_specs.append(
        pl.BlockSpec((arrived.shape[0], 1, block, width), lambda i: (0, jnp.maximum(i - lead, 0), 0, 0))
    )
    if summed is not None:
        operands.append(summed)
        in_specs.append(flat)
    total = jax.ShapeDtypeStruct((row_total, width), jnp.float32)
    out_shape, out_specs = total, flat
    if last:
        scale, panels = finish
        operands += [lax.axis_index("feat").astype(jnp.int32).reshape(1), scale]
        in_specs += [pl.BlockSpec(memory_space=pltpu.SMEM), flat]
        part = (row_total // panels, width)
        out_shape = [pltpu.HBM(part, jnp.bfloat16)] * panels
        out_shape.append(jax.ShapeDtypeStruct((row_total, width), jnp.bfloat16))
        out_specs = [pl.BlockSpec(part, lambda i: (0, 0))] * panels + [flat]
    return pl.pallas_call(
        body,
        grid=(arrived.shape[1] + lead,),
        out_shape=out_shape,
        in_specs=in_specs,
        out_specs=out_specs,
        scratch_shapes=[pltpu.VMEM((row_total, width), jnp.float32)] if last else [],
        compiler_params=pltpu.CompilerParams(vmem_limit_bytes=40 << 20),
        name="hop_last" if last else "hop_stage",
    )(*operands)


def shift(array, axis, step):
    length = lax.axis_size(axis)
    return lax.ppermute(array, axis, [(i, (i + step) % length) for i in range(length)])


def propagate(source, dense, wanted, scale, panels, block, cuts, beside):
    _, width = source.shape
    along = lax.axis_size(Z)
    far = along // 2
    own = source.reshape(-1, block, width)
    half = own.shape[0] // 2
    places, sources = [0], [own]
    low, high = own, own
    for distance in range(1, far):
        low, high = shift(low, Z, 1), shift(high, Z, -1)
        places += [distance, along - distance]
        sources += [high, low]
    opposite = shift(low[:half], Z, 1), shift(high[half:], Z, -1)
    places.append(far)
    sources.append(opposite)

    summed, done = None, ()
    for start, stop in zip([0] + cuts, cuts + [along]):
        outgoing = pick(places[start:stop], wanted, sources[start:stop])
        arrived = lax.all_to_all(outgoing, XC, split_axis=0, concat_axis=0, tiled=True)
        if stop == along and beside is not None:
            summed, done = lax.optimization_barrier((summed, beside()))
        base = start + 1 if start else 0
        summed = hop_stage(
            dense,
            base,
            None if start else own,
            arrived,
            summed,
            (scale, panels) if stop == along else None,
        )
    return summed, done


def gather_rows(rows):
    along, size = lax.axis_size(Z), lax.axis_size(XC)
    copies = jnp.broadcast_to(rows[None], (size, *rows.shape))
    own = lax.all_to_all(copies, XC, 0, 0, tiled=True).reshape(-1, rows.shape[1])
    position = lax.axis_index(Z)

    def put(whole, piece, index):
        return lax.dynamic_update_index_in_dim(whole, piece, index % whole.shape[0], 0)

    other = lax.ppermute(own, Z, [(i, i ^ 1) for i in range(along)])
    pair = jnp.zeros((2, *own.shape), own.dtype)
    pair = put(put(pair, own, position), other, position + 1)
    up, down = shift(pair, Z, 2), shift(pair, Z, -2)
    opposite = [shift(up[0], Z, 2), shift(down[1], Z, -2)]
    whole = jnp.zeros((along // 2, *pair.shape), own.dtype)
    position = position // 2
    whole = put(put(whole, pair, position), up, position - 1)
    whole = put(put(whole, down, position + 1), jnp.stack(opposite), position + 2)
    return whole.reshape(-1, rows.shape[1])


def at(array, index):
    return lax.dynamic_index_in_dim(array, index % array.shape[0], 0, keepdims=False)


def spread(near):
    return [near[0]] + [shift(near[i], "feat", i) for i in range(1, len(near))]


def term_of(owner_rows, owner_weight):
    return lax.dot_general(
        owner_rows, owner_weight, (((1,), (1,)), ((), ())), preferred_element_type=jnp.float32
    )


def layer(near, early, first_terms, last_weight, weight, out_bias, cotangent):
    along = lax.axis_size(Z)
    wide = jnp.concatenate(spread(near[-1]), axis=1)
    linear = first_terms + term_of(wide, last_weight)
    by_owner = [
        jnp.concatenate([early[i], near[-1][i]], axis=1) for i in range(len(early))
    ]
    linear = linear + out_bias[None, :]
    sigmoid_val = jax.nn.sigmoid(linear)
    output = (linear * sigmoid_val).astype(jnp.bfloat16)
    grad_linear = (
        cotangent.astype(jnp.float32) * sigmoid_val * (1.0 + linear * (1.0 - sigmoid_val))
    ).astype(jnp.bfloat16)

    bias = jnp.sum(grad_linear.astype(jnp.float32), axis=0)
    axes = ("node_1", "node_2", "feat")
    copies = jnp.broadcast_to(bias[None], (lax.axis_size(axes), bias.shape[0]))
    copies = lax.all_to_all(copies, axes, 0, 0, tiled=True)
    bias = jnp.sum(copies, axis=0)
    half = grad_linear.shape[0] // 2
    up, down = shift(grad_linear, "feat", 1), shift(grad_linear, "feat", -1)
    opposite = [shift(up[:half], "feat", 1), shift(down[half:], "feat", -1)]
    opposite = jnp.concatenate(opposite)

    def outer(grads, owner_rows):
        return lax.dot_general(
            grads, owner_rows, (((0,), (0,)), ((), ())), preferred_element_type=jnp.float32
        )

    grads = jnp.concatenate([grad_linear, up, down, opposite])
    term = outer(grads, jnp.concatenate([by_owner[i] for i in (0, 3, 1, 2)]))
    columns = term.shape[1]
    term = term.reshape(along, 4, 2, weight.shape[0], columns)
    core = lax.axis_index("node_2")
    mine = lax.dynamic_index_in_dim(term, core, 2, keepdims=False)
    other = jnp.moveaxis(lax.dynamic_index_in_dim(term, 1 - core, 2, keepdims=False), 1, 0)
    other = shift(other.astype(jnp.bfloat16), "node_2", 1)
    term = (jnp.moveaxis(mine, 1, 0) + other.astype(jnp.float32)).astype(jnp.bfloat16)
    term = lax.all_to_all(term.reshape(4, -1, columns), "node_1", 0, 0, tiled=True)
    term = jnp.sum(term.astype(jnp.float32), axis=0).astype(jnp.bfloat16)
    high = lax.reduce_precision(bias, exponent_bits=8, mantissa_bits=7)
    pair = jnp.concatenate([high, bias - high]).astype(jnp.bfloat16)
    extra = jnp.pad(pair, (0, 8 * columns - 2 * bias.shape[0]))
    extra = jnp.broadcast_to(extra.reshape(1, 8, columns), (along, 8, columns))
    term = jnp.concatenate([term.reshape(along, -1, columns), extra], axis=1)
    term = lax.all_to_all(term, Z, 0, 0, tiled=True)
    term = jnp.sum(term.astype(jnp.float32), axis=0)
    weight_grad = term[:-8].reshape(weight.shape)
    pair = term[-8:].reshape(-1)[: 2 * bias.shape[0]].reshape(2, -1)
    bias = pair[0] + pair[1]
    return (output, weight_grad, bias)


def local(
    features,
    degrees,
    tile_row,
    tile_col,
    tile_count,
    send_block,
    tile_val,
    weight,
    out_bias,
    cotangent,
):
    rows, panel = features.shape
    block = tile_val.shape[-1]
    row_blocks = rows // block
    parts = send_block.shape[0]
    along = lax.axis_size(Z)
    across = parts // along
    z_index = lax.axis_index(Z)
    xc_index = lax.axis_index(XC)

    panels = lax.axis_size("feat")
    feat_index = lax.axis_index("feat")
    row_scale = lax.rsqrt(degrees.astype(jnp.float32))[:, None]
    source = (features * row_scale).astype(jnp.bfloat16)
    scale = jnp.broadcast_to(row_scale, (rows, panel))

    by_place = send_block.reshape(along, across, along, across)
    mine = lax.dynamic_index_in_dim(by_place, xc_index, 1, keepdims=False)
    mine = lax.dynamic_index_in_dim(mine, z_index, 1, keepdims=False)
    wanted = jnp.roll(mine, -z_index, axis=0)

    order = [0]
    for distance in range(1, along // 2):
        order += [distance, along - distance]
    order.append(along // 2)
    place_of = jnp.array([order.index(offset) for offset in range(along)], dtype=jnp.int32)
    sender = jnp.maximum(tile_col[0] - row_blocks, 0)
    offset = (sender // across - z_index) % along
    remote = GROUP + place_of[offset] * across + sender % across
    slots = jnp.where(tile_col[0] < row_blocks, tile_col[0], remote)
    dense = densify(tile_row[0], slots, tile_count, tile_val[0], GROUP + parts, rows)

    owned = features.astype(jnp.bfloat16).reshape(panels, rows // panels, panel)
    near = [[at(owned, feat_index + i) for i in range(panels)]]
    flat_weight = gather_rows(weight.reshape(weight.shape[0], -1))
    (*hop, source), _ = propagate(source, dense, wanted, scale, panels, block, [3], None)
    near.append(hop)
    early = [jnp.concatenate([near[0][i], near[1][i]], axis=1) for i in range(panels)]
    half = flat_weight.shape[0] // 2
    up, down = shift(flat_weight, "feat", 1), shift(flat_weight, "feat", -1)
    opposite = [shift(up[:half], "feat", 1), shift(down[half:], "feat", -1)]
    by_panel = [flat_weight, up, jnp.concatenate(opposite), down]

    def beside():
        terms = 0.0
        for rows_wide, panel_weight in zip(spread(early), by_panel):
            terms = terms + term_of(rows_wide, panel_weight[:, : 2 * panel])
        last_weight = jnp.concatenate([piece[:, 2 * panel :] for piece in by_panel], axis=1)
        return terms, last_weight

    (*hop, _), (first_terms, last_weight) = propagate(
        source, dense, wanted, scale, panels, block, [3], beside
    )
    near.append(hop)

    return layer(near, early, first_terms, last_weight, weight, out_bias, cotangent)


def solution(mesh):
    split = Mesh(
        mesh.devices.reshape(8, 4, 2, mesh.shape["feat"]), ("node_0", "node_1", "node_2", "feat")
    )
    return jax.shard_map(
        local,
        mesh=split,
        in_specs=(
            P(NODE, "feat"),
            P(NODE),
            P(NODE, None),
            P(NODE, None),
            P(NODE),
            P(),
            P(NODE, None, None, None),
            P(NODE, None, "feat"),
            P(),
            P(NODE_FEAT, None),
        ),
        out_specs=(P(NODE_FEAT, None), P(NODE, None, "feat"), P()),
        check_vma=False,
    )
```
